256 devices in a mesh: section: 4 (over x), seq: 64 (over y, z, core).
Axes of the slice: x: 4, y: 4, z: 8, core: 2. Of those that a mesh axis runs over, the one named last changes fastest.
Arguments:
- layer_input: bfloat16 [4, 4, 4096, 1536], P('section', None, 'seq'), may hold values from -16 to 16
- grad_top: bfloat16 [4, 4096, 1536], P(None, 'seq'), may hold values from -16 to 16
- w_conv: bfloat16 [4, 1536, 2304], P('section'), may hold values from -0.09375 to 0.09375
- w_out: bfloat16 [4, 1536, 768], P('section'), may hold values from -0.21875 to 0.21875
Outputs:
- grad_inputs: bfloat16 [4, 4, 4096, 1536], P('section', None, 'seq')
- w_conv_grad: float32 [4, 1536, 2304], P('section', 'seq')
- w_out_grad: float32 [4, 1536, 768], P('section', 'seq')
The draws below stay inside these ranges and needn't reach their ends.
All inputs are finite; a program needn't handle non-finite values.
Results may differ from the reference program's by a relative error of at most 0.007.
Values may be sent and summed in bfloat16 or wider, within the bound.
A program may use at most 128 MiB of HBM per device.

```python
import math
import jax
import jax.numpy as jnp

C = 1536
F = 768
SEQS = 4
DMAX = 64
L = 4096
LAYERS = 4
N_SECTION = 4


def raised(values, stream_key, source, target, blocks, factor):
    def block_of(position):
        return (jnp.arange(values.shape[position]) // (values.shape[position] // blocks)).reshape((-1,) + (1,) * (values.ndim - 1 - position))

    first = jax.random.permutation(stream_key, blocks)[block_of(target)]
    other_side = (block_of(target) + blocks // 2) % blocks
    return jnp.where((block_of(source) == first) | (block_of(source) == other_side), factor * values, values)


def block_scale(stream_key, extent, split, smallest, high):
    gain = 1.0
    for dim, blocks in split:
        heights = jax.random.uniform(jax.random.fold_in(jax.random.fold_in(stream_key, 6), dim), (blocks,), jnp.float32, smallest / len(split), high / len(split))
        gain = gain * jnp.repeat(jnp.exp(heights), extent[dim] // blocks).reshape((-1,) + (1,) * (len(extent) - 1 - dim))
    return gain


def gaussian(own_key, shape, spread, most, shards=(), kind=jnp.bfloat16):
    drawn = spread * jax.random.normal(own_key, shape, jnp.float32)
    if shards:
        drawn = drawn * block_scale(own_key, shape, shards, -0.22, 0.18)
    return jnp.clip(drawn, -most, most).astype(kind)


def noise_with(stream_key, dims, deviation, reach, shards, heavy, held_as=jnp.bfloat16):
    array = deviation * jax.random.normal(stream_key, dims, jnp.float32)
    if shards:
        array = array * block_scale(stream_key, dims, shards, -0.22, 0.18)
    return jnp.clip(raised(array, jax.random.fold_in(stream_key, 3), *heavy), -reach, reach).astype(held_as)


def setup_inputs(seed: int = 0) -> dict:
    streams_of = jax.random.split(jax.random.key(seed), 5)
    layer_input = noise_with(streams_of[0], (LAYERS, SEQS, L, C), 1.0, 16.0, ((0, 4), (2, 64)), (2, 3, 64, 4.0))
    grad_top = noise_with(streams_of[1], (SEQS, L, C), 1.0, 16.0, ((1, 64),), (1, 2, 64, 4.0))
    w_conv = gaussian(streams_of[2], (LAYERS, C, 3 * F), (3 * C) ** -0.5, 0.09375, ((0, 4),))
    w_out = gaussian(streams_of[3], (LAYERS, C, F), F ** -0.5, 0.21875, ((0, 4),))
    return {"layer_input": layer_input, "grad_top": grad_top, "w_conv": w_conv, "w_out": w_out}


def gelu_slope(value):
    return 0.5 * (1.0 + jax.scipy.special.erf(value * 0.7071067811865476)) + value * jnp.exp(-0.5 * value * value) * 0.3989422804014327

def reference(layer_input, grad_top, w_conv, w_out):
    length = layer_input.shape[2]
    width = w_out.shape[2]
    scale = 1.0 / math.sqrt(SEQS * length)
    base = DMAX // 2 ** (N_SECTION - 1)
    incoming = grad_top
    grads_in = []
    grads_conv = []
    grads_out = []
    for section in reversed(range(N_SECTION)):
        dilation = base * 2 ** section
        inputs = layer_input[section]
        kernel = w_conv[section].astype(jnp.float32)
        project = w_out[section].astype(jnp.float32)
        hidden = jax.nn.gelu(inputs.astype(jnp.float32), approximate=False).astype(jnp.bfloat16)
        padded = jnp.pad(hidden, ((0, 0), (DMAX, DMAX), (0, 0))).astype(jnp.float32)
        pre = jnp.zeros((SEQS, length, width), jnp.float32)
        windows = []
        for tap in range(3):
            start = DMAX + (tap - 1) * dilation
            window = padded[:, start:start + length]
            windows.append(window)
            pre = pre + jnp.einsum('bpc,cf->bpf', window, kernel[:, tap * width:(tap + 1) * width])
        gated = jax.nn.gelu(pre, approximate=False).astype(jnp.bfloat16)
        cot = incoming.astype(jnp.float32)
        dgate = jnp.einsum('bpc,cf->bpf', cot, project)
        dpre = (dgate * gelu_slope(pre)).astype(jnp.bfloat16)
        dpad = jnp.pad(dpre, ((0, 0), (DMAX, DMAX), (0, 0))).astype(jnp.float32)
        dhidden = jnp.zeros((SEQS, length, w_conv.shape[1]), jnp.float32)
        for tap in range(3):
            start = DMAX - (tap - 1) * dilation
            dhidden = dhidden + jnp.einsum('bpf,cf->bpc', dpad[:, start:start + length], kernel[:, tap * width:(tap + 1) * width])
        dinput = (cot + dhidden * gelu_slope(inputs.astype(jnp.float32))).astype(jnp.bfloat16)
        dpre_f = dpre.astype(jnp.float32)
        conv_grad = jnp.concatenate([jnp.einsum('bpc,bpf->cf', windows[tap], dpre_f) for tap in range(3)], axis=1) * scale
        out_grad = jnp.einsum('bpc,bpf->cf', cot, gated.astype(jnp.float32)) * scale
        grads_in.append(dinput)
        grads_conv.append(conv_grad)
        grads_out.append(out_grad)
        incoming = dinput
    grads_in = grads_in[::-1]
    grads_conv = grads_conv[::-1]
    grads_out = grads_out[::-1]
    return (jnp.stack(grads_in), jnp.stack(grads_conv), jnp.stack(grads_out))
```

```python
import functools
import math

import jax
import jax.numpy as jnp
from jax import lax
from jax.experimental import pallas as pl
from jax.experimental.pallas import tpu as pltpu
from jax.sharding import PartitionSpec as P

BF = jnp.bfloat16
F32 = jnp.float32
NY, NZ = 4, 8
RB = 48
HW = 384


def seq_place():
    j = lax.axis_index("seq")
    c = lax.rem(j, 2)
    z = lax.rem(lax.div(j, 2), NZ)
    y = lax.div(j, 2 * NZ)
    return y, z, c


def seq_at(y, z, c):
    return (y * NZ + z) * 2 + c


def ring_bufs(n, nb, wd):
    hn = n // 2
    wu = HW - wd
    out = []
    for _ in range(2):
        out += [
            pltpu.VMEM((nb, RB, wd), BF),
            pltpu.VMEM((nb, RB, wu), BF),
            pltpu.VMEM((hn - 1, nb, RB, HW), BF),
            pltpu.VMEM((hn - 1, nb, RB, HW), BF),
        ]
    return out


class Ring:
    def __init__(self, n, nb, wd, me, down, up, index, block, refs, sems, first):
        self.n, self.nb, self.wd, self.me = n, nb, wd, me
        self.down, self.up, self.index, self.block = down, up, index, block
        self.s0d, self.s0u, self.sd, self.su, self.r0d, self.r0u, self.rd, self.ru = refs
        self.send, self.recv = sems
        self.first = first
        self.copies = []
        self.last = None

    def copy(self, src, dst, to):
        k = self.first + len(self.copies)
        one = pltpu.make_async_remote_copy(
            src_ref=src, dst_ref=dst, send_sem=self.send.at[k], recv_sem=self.recv.at[k],
            device_id={"seq": to}, device_id_type=pl.DeviceIdType.MESH)
        one.start()
        self.copies.append(one)
        return one

    def each(self, body):
        if self.nb == 1:
            body(0)
        else:
            lax.fori_loop(0, self.nb, lambda k, t: (body(k), t)[1], 0)

    def start(self):
        dest = lax.rem(self.me + self.n // 2, self.n)
        wd = self.wd

        def body(k):
            own = self.block[self.index(k, dest)]
            self.s0d[k] = own[:, :wd].astype(BF)
            self.s0u[k] = own[:, wd:].astype(BF)

        self.each(body)
        self.last = (self.copy(self.s0d, self.r0d, self.down), self.copy(self.s0u, self.r0u, self.up))

    def step(self, i):
        away = self.n // 2 - i
        wd = self.wd
        dest_d = lax.rem(self.me + self.n - away, self.n)
        dest_u = lax.rem(self.me + away, self.n)
        prev_d, prev_u = self.last
        prev_d.wait_recv()

        def body_d(k):
            own = self.block[self.index(k, dest_d)]
            if i == 1:
                self.sd[i - 1, k, :, :wd] = (own[:, :wd] + self.r0d[k].astype(F32)).astype(BF)
                self.sd[i - 1, k, :, wd:] = own[:, wd:].astype(BF)
            else:
                self.sd[i - 1, k] = (own + self.rd[i - 2, k].astype(F32)).astype(BF)

        self.each(body_d)
        new_d = self.copy(self.sd.at[i - 1], self.rd.at[i - 1], self.down)
        prev_u.wait_recv()

        def body_u(k):
            own = self.block[self.index(k, dest_u)]
            if i == 1:
                self.su[i - 1, k, :, :wd] = own[:, :wd].astype(BF)
                self.su[i - 1, k, :, wd:] = (own[:, wd:] + self.r0u[k].astype(F32)).astype(BF)
            else:
                self.su[i - 1, k] = (own + self.ru[i - 2, k].astype(F32)).astype(BF)

        self.each(body_u)
        new_u = self.copy(self.su.at[i - 1], self.ru.at[i - 1], self.up)
        self.last = (new_d, new_u)

    def finish(self):
        end = self.n // 2 - 2
        for one in self.last:
            one.wait_recv()

        def body(k):
            at = self.index(k, self.me)
            self.block[at] = self.block[at] + (self.rd[end, k].astype(F32) + self.ru[end, k].astype(F32))

        self.each(body)

    def drain(self):
        for one in self.copies:
            one.wait_send()


ORDERS = ("zy", "zy", "yz", "yz")
SPLITS = (256, 128, 256, 128)


def rs_scratch():
    shapes = [pltpu.VMEM((NY, NZ, RB, HW), F32) for _ in range(4)]
    for order, wd in zip(ORDERS, SPLITS):
        if order == "zy":
            shapes += ring_bufs(NZ, NY, wd) + ring_bufs(NY, 1, wd)
        else:
            shapes += ring_bufs(NY, NZ, wd) + ring_bufs(NZ, 1, wd)
    shapes += [
        pltpu.VMEM((4, RB // 2, HW), F32),
        pltpu.VMEM((4, RB // 2, HW), F32),
        pltpu.SemaphoreType.DMA((49,)),
        pltpu.SemaphoreType.DMA((49,)),
    ]
    return shapes


def rs_run(fill, scale, conv_ref, out_ref, refs):
    y, z, c = seq_place()
    blocks = refs[:4]
    bufs = refs[4:4 + 64]
    xs, xr, send, recv = refs[68:72]
    zd, zu = seq_at(y, lax.rem(z + NZ - 1, NZ), c), seq_at(y, lax.rem(z + 1, NZ), c)
    yd, yu = seq_at(lax.rem(y + NY - 1, NY), z, c), seq_at(lax.rem(y + 1, NY), z, c)
    plans = []
    first = 0
    for b in range(4):
        block = blocks[b]
        one, two = bufs[16 * b:16 * b + 8], bufs[16 * b + 8:16 * b + 16]
        wd = SPLITS[b]
        if ORDERS[b] == "zy":
            r1 = Ring(NZ, NY, wd, z, zd, zu, lambda k, d: (k, d), block, one, (send, recv), first)
            r2 = Ring(NY, 1, wd, y, yd, yu, lambda k, d: (d, z), block, two, (send, recv), first + 8)
            plan = [functools.partial(r1.step, i) for i in (1, 2, 3)]
            plan += [lambda r1=r1, r2=r2: (r1.finish(), r2.start()), functools.partial(r2.step, 1), r2.finish]
        else:
            r1 = Ring(NY, NZ, wd, y, yd, yu, lambda k, d: (d, k), block, one, (send, recv), first)
            r2 = Ring(NZ, 1, wd, z, zd, zu, lambda k, d: (y, d), block, two, (send, recv), first + 4)
            plan = [functools.partial(r1.step, 1), lambda r1=r1, r2=r2: (r1.finish(), r2.start())]
            plan += [functools.partial(r2.step, i) for i in (1, 2, 3)] + [r2.finish]
        first += 12
        plans.append((r1, r2, plan))
    for b in (0, 2, 1, 3):
        fill(b, blocks[b])
        plans[b][0].start()
    for k in range(6):
        for b in (0, 2, 1, 3):
            plans[b][2][k]()
    half = RB // 2
    for b in range(4):
        xs[b] = blocks[b][y, z, pl.ds(pl.multiple_of((1 - c) * half, 8), half), :]
    swap = pltpu.make_async_remote_copy(
        src_ref=xs, dst_ref=xr, send_sem=send.at[48], recv_sem=recv.at[48],
        device_id={"seq": seq_at(y, z, 1 - c)}, device_id_type=pl.DeviceIdType.MESH)
    swap.start()

    def put(b, core, value):
        at = pl.multiple_of(core * HW, 128)
        if b == 3:
            out_ref[:, pl.ds(at, HW)] = value * scale
        else:
            conv_ref[:, pl.ds(pl.multiple_of(b * 2 * HW + at, 128), HW)] = value * scale

    for b in range(4):
        put(b, c, blocks[b][y, z, pl.ds(pl.multiple_of(c * half, 8), half), :])
    swap.wait_recv()
    for b in range(4):
        put(b, 1 - c, xr[b])
    swap.wait_send()
    for r1, r2, _ in plans:
        r1.drain()
        r2.drain()


def grads_kernel(rows, scale, h_hbm, cot_hbm, dwin_hbm, g_hbm, conv_ref, out_ref, hx, ct, dw, gg, hT, cT, xsend, xrecv, local, *refs):
    y, z, c = seq_place()
    partner = seq_at(y, z, 1 - c)
    barrier = pltpu.get_barrier_semaphore()
    for to in (partner,
               seq_at(y, lax.rem(z + NZ - 1, NZ), c), seq_at(y, lax.rem(z + 1, NZ), c),
               seq_at(lax.rem(y + NY - 1, NY), z, c), seq_at(lax.rem(y + 1, NY), z, c)):
        pl.semaphore_signal(barrier, inc=1, device_id={"seq": to}, device_id_type=pl.DeviceIdType.MESH)
    pl.semaphore_wait(barrier, 5)
    top, low = pl.ds(0, rows), pl.ds(rows, rows)
    away, mine = [], []

    def remote(src, dst):
        k = len(away)
        one = pltpu.make_async_remote_copy(
            src_ref=src, dst_ref=dst, send_sem=xsend.at[k], recv_sem=xrecv.at[k],
            device_id={"seq": partner}, device_id_type=pl.DeviceIdType.MESH)
        one.start()
        away.append(one)

    def near(src, dst):
        one = pltpu.make_async_copy(src, dst, local.at[len(mine)])
        one.start()
        mine.append(one)

    def cols(t, core):
        return pl.ds(pl.multiple_of(t * 2 * HW + core * HW, 128), HW)

    near(h_hbm, hx.at[top])
    remote(h_hbm, hx.at[low])
    for t in range(3):
        near(dwin_hbm.at[:, cols(t, c)], dw.at[top, pl.ds(t * HW, HW)])
        remote(dwin_hbm.at[:, cols(t, 1 - c)], dw.at[low, pl.ds(t * HW, HW)])
    near(g_hbm.at[:, cols(0, c)], gg.at[top])
    remote(g_hbm.at[:, cols(0, 1 - c)], gg.at[low])
    near(cot_hbm, ct.at[top])
    remote(cot_hbm, ct.at[low])

    def turn(src, dst, half):
        for m in range(NY):
            dst[m, :, half * rows:(half + 1) * rows] = src[half * rows:(half + 1) * rows, m * HW:(m + 1) * HW].T

    mine[0].wait()
    turn(hx, hT, 0)
    mine[5].wait()
    turn(ct, cT, 0)
    away[0].wait_recv()
    turn(hx, hT, 1)
    for k in (1, 2, 3):
        mine[k].wait()
        away[k].wait_recv()
    away[5].wait_recv()
    turn(ct, cT, 1)
    mine[4].wait()
    away[4].wait_recv()

    def fill(b, block):
        lhs = cT if b == 3 else hT
        for m in range(NY):
            rhs = gg[...] if b == 3 else dw[:, b * HW:(b + 1) * HW]
            got = jnp.dot(lhs[m], rhs, preferred_element_type=F32)
            block[m] = got.reshape(NZ, RB, HW)

    rs_run(fill, scale, conv_ref, out_ref, refs)
    for one in away:
        one.wait_send()


def grads_call(h, cot, dwin, g, scale):
    rows = h.shape[0]
    scratch = [
        pltpu.VMEM((2 * rows, 1536), BF), pltpu.VMEM((2 * rows, 1536), BF),
        pltpu.VMEM((2 * rows, 3 * HW), BF), pltpu.VMEM((2 * rows, HW), BF),
        pltpu.VMEM((NY, HW, 2 * rows), BF), pltpu.VMEM((NY, HW, 2 * rows), BF),
        pltpu.SemaphoreType.DMA((6,)), pltpu.SemaphoreType.DMA((6,)), pltpu.SemaphoreType.DMA((6,)),
    ] + rs_scratch()
    return pl.pallas_call(
        functools.partial(grads_kernel, rows, scale),
        out_shape=(jax.ShapeDtypeStruct((24, 2304), F32), jax.ShapeDtypeStruct((24, 768), F32)),
        in_specs=[pl.BlockSpec(memory_space=pl.ANY)] * 4,
        out_specs=(pl.BlockSpec(memory_space=pltpu.VMEM), pl.BlockSpec(memory_space=pltpu.VMEM)),
        scratch_shapes=scratch,
        compiler_params=pltpu.CompilerParams(collective_id=1, has_side_effects=True, vmem_limit_bytes=62 << 20),
    )(h, cot, dwin, g)


DMAX = 64


def shifted(value, axis, by):
    peers = lax.axis_size(axis)
    pairs = [(i, i + by) for i in range(peers) if 0 <= i + by < peers]
    return lax.ppermute(value, axis, pairs)


def padded(cells, sides, width):
    for axis, dim in sides:
        count = lax.axis_size(axis)
        ends = count - 1
        head = lax.slice_in_dim(cells, 0, width, axis=dim)
        tail = lax.slice_in_dim(cells, cells.shape[dim] - width, cells.shape[dim], axis=dim)
        cells = jnp.concatenate(
            [
                lax.ppermute(tail, axis, [(i, (i + 1) % count) for i in range(ends)]),
                cells,
                lax.ppermute(head, axis, [((i + 1) % count, i) for i in range(ends)]),
            ],
            axis=dim,
        )
    return cells


def gelu_slope(value):
    return (
        0.5 * (1.0 + jax.scipy.special.erf(value * 0.7071067811865476))
        + value * jnp.exp(-0.5 * value * value) * 0.3989422804014327
    )


def put_piece(store, value, first, valid):
    current = lax.dynamic_slice_in_dim(store, first, value.shape[0], 0)
    fresh = jnp.where(valid, value, current)
    return lax.dynamic_update_slice_in_dim(store, fresh, first, 0)


def body(layer_input, grad_top, w_conv, w_out):
    sections = lax.axis_size("section")
    section = lax.axis_index("section")
    seq_count = lax.axis_size("seq")
    seqs_all, positions, chans = grad_top.shape
    width = w_out.shape[2]
    base = DMAX // 2 ** (sections - 1)
    dilation = base * jnp.left_shift(jnp.int32(1), section)
    acts = layer_input[0]
    kernel = w_conv[0]
    project = w_out[0]
    pieces = 2
    span = seqs_all // pieces
    steps = pieces + sections - 1
    rim_store = jnp.zeros((seqs_all, positions, chans), jnp.bfloat16)
    slope_store = jnp.zeros((seqs_all, positions, 3 * width), jnp.bfloat16)
    gate_store = jnp.zeros((seqs_all, positions, width), jnp.bfloat16)
    cot_store = jnp.zeros((seqs_all, positions, chans), jnp.bfloat16)
    input_store = jnp.zeros((seqs_all, positions, chans), jnp.bfloat16)
    previous = jnp.zeros((span, positions, chans), jnp.bfloat16)
    for step in range(steps):
        piece = step - (sections - 1 - section)
        valid = jnp.logical_and(piece >= 0, piece < pieces)
        first = jnp.clip(piece, 0, pieces - 1) * span
        if step == 0:
            received = jnp.zeros((span, positions, chans), jnp.bfloat16)
        else:
            received = shifted(previous, "section", -1)
        top = lax.dynamic_slice_in_dim(grad_top, first, span, 0)
        incoming = jnp.where(section == sections - 1, top, received)
        inputs = lax.dynamic_slice_in_dim(acts, first, span, 0)
        hidden = jax.nn.gelu(inputs.astype(jnp.float32), approximate=False).astype(jnp.bfloat16)
        extended = padded(hidden, (("seq", 1),), DMAX)
        pre = jnp.zeros((span, positions, width), jnp.float32)
        for tap in range(3):
            window = lax.dynamic_slice_in_dim(extended, DMAX + (tap - 1) * dilation, positions, 1)
            pre = pre + jnp.einsum(
                "bpc,cf->bpf",
                window,
                kernel[:, tap * width : (tap + 1) * width],
                preferred_element_type=jnp.float32,
            )
        gated = jax.nn.gelu(pre, approximate=False).astype(jnp.bfloat16)
        dgate = jnp.einsum("bpc,cf->bpf", incoming, project, preferred_element_type=jnp.float32)
        dpre = (dgate * gelu_slope(pre)).astype(jnp.bfloat16)
        dpre_wide = padded(dpre, (("seq", 1),), DMAX)
        dhidden = jnp.zeros((span, positions, chans), jnp.float32)
        windows = []
        for tap in range(3):
            window = lax.dynamic_slice_in_dim(dpre_wide, DMAX - (tap - 1) * dilation, positions, 1)
            windows.append(window)
            dhidden = dhidden + jnp.einsum(
                "bpf,cf->bpc",
                window,
                kernel[:, tap * width : (tap + 1) * width],
                preferred_element_type=jnp.float32,
            )
        dinput = (
            incoming.astype(jnp.float32) + dhidden * gelu_slope(inputs.astype(jnp.float32))
        ).astype(jnp.bfloat16)
        rim_store = put_piece(rim_store, hidden, first, valid)
        slope_store = put_piece(slope_store, jnp.concatenate(windows, axis=2), first, valid)
        gate_store = put_piece(gate_store, gated, first, valid)
        cot_store = put_piece(cot_store, incoming, first, valid)
        input_store = put_piece(input_store, dinput, first, valid)
        previous = dinput
    scale = 1.0 / math.sqrt(seqs_all * positions * seq_count)
    rows = seqs_all * positions
    conv_grad, out_grad = grads_call(
        rim_store.reshape(rows, chans), cot_store.reshape(rows, chans),
        slope_store.reshape(rows, 3 * width), gate_store.reshape(rows, width), scale)
    return (input_store[None], conv_grad[None], out_grad[None])


def solution(mesh):
    return jax.shard_map(
        body,
        mesh=mesh,
        in_specs=(
            P("section", None, "seq", None),
            P(None, "seq", None),
            P("section", None, None),
            P("section", None, None),
        ),
        out_specs=(
            P("section", None, "seq", None),
            P("section", "seq", None),
            P("section", "seq", None),
        ),
        check_vma=False,
    )
```

```python
import functools
import math

import jax
import jax.numpy as jnp
from jax import lax
from jax.experimental import pallas as pl
from jax.experimental.pallas import tpu as pltpu
from jax.sharding import PartitionSpec as P

BF = jnp.bfloat16
F32 = jnp.float32
NY, NZ = 4, 8
RB = 48
HW = 384


def seq_place():
    j = lax.axis_index("seq")
    c = lax.rem(j, 2)
    z = lax.rem(lax.div(j, 2), NZ)
    y = lax.div(j, 2 * NZ)
    return y, z, c


def seq_at(y, z, c):
    return (y * NZ + z) * 2 + c


SEQS = 4
PB = 64
CH = 1536
FW = 768
DMAX = 64
NS = 4
NQ = 3
QW = CH // NQ


def ring_bufs(n, nb, wd):
    hn = n // 2
    wu = HW - wd
    out = []
    for _ in range(2):
        out += [
            pltpu.VMEM((nb, RB, wd), BF),
            pltpu.VMEM((nb, RB, wu), BF),
            pltpu.VMEM((hn - 1, nb, RB, HW), BF),
            pltpu.VMEM((hn - 1, nb, RB, HW), BF),
        ]
    return out


class Ring:
    def __init__(self, n, nb, wd, me, down, up, index, block, refs, sems, first):
        self.n, self.nb, self.wd, self.me = n, nb, wd, me
        self.down, self.up, self.index, self.block = down, up, index, block
        self.s0d, self.s0u, self.sd, self.su, self.r0d, self.r0u, self.rd, self.ru = refs
        self.send, self.recv = sems
        self.first = first
        self.copies = []
        self.last = None

    def copy(self, src, dst, to):
        k = self.first + len(self.copies)
        one = pltpu.make_async_remote_copy(
            src_ref=src, dst_ref=dst, send_sem=self.send.at[k], recv_sem=self.recv.at[k],
            device_id={"seq": to}, device_id_type=pl.DeviceIdType.MESH)
        one.start()
        self.copies.append(one)
        return one

    def each(self, body):
        if self.nb == 1:
            body(0)
        else:
            lax.fori_loop(0, self.nb, lambda k, t: (body(k), t)[1], 0)

    def start(self):
        dest = lax.rem(self.me + self.n // 2, self.n)
        wd = self.wd

        def body(k):
            own = self.block[self.index(k, dest)]
            self.s0d[k] = own[:, :wd].astype(BF)
            self.s0u[k] = own[:, wd:].astype(BF)

        self.each(body)
        self.last = (self.copy(self.s0d, self.r0d, self.down), self.copy(self.s0u, self.r0u, self.up))

    def step(self, i):
        away = self.n // 2 - i
        wd = self.wd
        dest_d = lax.rem(self.me + self.n - away, self.n)
        dest_u = lax.rem(self.me + away, self.n)
        prev_d, prev_u = self.last
        prev_d.wait_recv()

        def body_d(k):
            own = self.block[self.index(k, dest_d)]
            if i == 1:
                self.sd[i - 1, k, :, :wd] = (own[:, :wd] + self.r0d[k].astype(F32)).astype(BF)
                self.sd[i - 1, k, :, wd:] = own[:, wd:].astype(BF)
            else:
                self.sd[i - 1, k] = (own + self.rd[i - 2, k].astype(F32)).astype(BF)

        self.each(body_d)
        new_d = self.copy(self.sd.at[i - 1], self.rd.at[i - 1], self.down)
        prev_u.wait_recv()

        def body_u(k):
            own = self.block[self.index(k, dest_u)]
            if i == 1:
                self.su[i - 1, k, :, :wd] = own[:, :wd].astype(BF)
                self.su[i - 1, k, :, wd:] = (own[:, wd:] + self.r0u[k].astype(F32)).astype(BF)
            else:
                self.su[i - 1, k] = (own + self.ru[i - 2, k].astype(F32)).astype(BF)

        self.each(body_u)
        new_u = self.copy(self.su.at[i - 1], self.ru.at[i - 1], self.up)
        self.last = (new_d, new_u)

    def finish(self):
        end = self.n // 2 - 2
        for one in self.last:
            one.wait_recv()

        def body(k):
            at = self.index(k, self.me)
            self.block[at] = self.block[at] + (self.rd[end, k].astype(F32) + self.ru[end, k].astype(F32))

        self.each(body)

    def drain(self):
        for one in self.copies:
            one.wait_send()


ORDERS = ("zy", "zy", "yz", "yz")
SPLITS = (256, 128, 256, 128)


def rs_scratch():
    shapes = [pltpu.VMEM((NY, NZ, RB, HW), F32) for _ in range(4)]
    for order, wd in zip(ORDERS, SPLITS):
        if order == "zy":
            shapes += ring_bufs(NZ, NY, wd) + ring_bufs(NY, 1, wd)
        else:
            shapes += ring_bufs(NY, NZ, wd) + ring_bufs(NZ, 1, wd)
    shapes += [
        pltpu.VMEM((4, RB // 2, HW), F32),
        pltpu.VMEM((4, RB // 2, HW), F32),
        pltpu.SemaphoreType.DMA((49,)),
        pltpu.SemaphoreType.DMA((49,)),
    ]
    return shapes


def rs_run(fill, scale, conv_ref, out_ref, refs):
    y, z, c = seq_place()
    blocks = refs[:4]
    bufs = refs[4:4 + 64]
    xs, xr, send, recv = refs[68:72]
    zd, zu = seq_at(y, lax.rem(z + NZ - 1, NZ), c), seq_at(y, lax.rem(z + 1, NZ), c)
    yd, yu = seq_at(lax.rem(y + NY - 1, NY), z, c), seq_at(lax.rem(y + 1, NY), z, c)
    plans = []
    first = 0
    for b in range(4):
        block = blocks[b]
        one, two = bufs[16 * b:16 * b + 8], bufs[16 * b + 8:16 * b + 16]
        wd = SPLITS[b]
        if ORDERS[b] == "zy":
            r1 = Ring(NZ, NY, wd, z, zd, zu, lambda k, d: (k, d), block, one, (send, recv), first)
            r2 = Ring(NY, 1, wd, y, yd, yu, lambda k, d: (d, z), block, two, (send, recv), first + 8)
            plan = [functools.partial(r1.step, i) for i in (1, 2, 3)]
            plan += [lambda r1=r1, r2=r2: (r1.finish(), r2.start()), functools.partial(r2.step, 1), r2.finish]
        else:
            r1 = Ring(NY, NZ, wd, y, yd, yu, lambda k, d: (d, k), block, one, (send, recv), first)
            r2 = Ring(NZ, 1, wd, z, zd, zu, lambda k, d: (y, d), block, two, (send, recv), first + 4)
            plan = [functools.partial(r1.step, 1), lambda r1=r1, r2=r2: (r1.finish(), r2.start())]
            plan += [functools.partial(r2.step, i) for i in (1, 2, 3)] + [r2.finish]
        first += 12
        plans.append((r1, r2, plan))
    for b in (0, 2, 1, 3):
        fill(b, blocks[b])
        plans[b][0].start()
    for k in range(6):
        for b in (0, 2, 1, 3):
            plans[b][2][k]()
    half = RB // 2
    for b in range(4):
        xs[b] = blocks[b][y, z, pl.ds(pl.multiple_of((1 - c) * half, 8), half), :]
    swap = pltpu.make_async_remote_copy(
        src_ref=xs, dst_ref=xr, send_sem=send.at[48], recv_sem=recv.at[48],
        device_id={"seq": seq_at(y, z, 1 - c)}, device_id_type=pl.DeviceIdType.MESH)
    swap.start()

    def put(b, core, value):
        at = pl.multiple_of(core * HW, 128)
        if b == 3:
            out_ref[:, pl.ds(at, HW)] = value * scale
        else:
            conv_ref[:, pl.ds(pl.multiple_of(b * 2 * HW + at, 128), HW)] = value * scale

    for b in range(4):
        put(b, c, blocks[b][y, z, pl.ds(pl.multiple_of(c * half, 8), half), :])
    swap.wait_recv()
    for b in range(4):
        put(b, 1 - c, xr[b])
    swap.wait_send()
    for r1, r2, _ in plans:
        r1.drain()
        r2.drain()


def remote(src, dst, send, recv, to):
    return pltpu.make_async_remote_copy(
        src_ref=src, dst_ref=dst, send_sem=send, recv_sem=recv,
        device_id=to, device_id_type=pl.DeviceIdType.MESH)


def gelu_parts(v):
    cdf = 0.5 * (1.0 + lax.erf(v * 0.7071067811865476))
    return v * cdf, cdf + v * jnp.exp(-0.5 * v * v) * 0.3989422804014327


def loop(n, body):
    lax.fori_loop(0, n, lambda i, t: (body(i), t)[1], 0)


NAMES = (
    ("xv", (SEQS, PB, CH), BF), ("wc", (CH, 3 * FW), BF), ("wo", (CH, FW), BF),
    ("hx", (SEQS, 2, PB, CH), BF), ("ho", (SEQS, PB, CH), BF), ("gx", (SEQS, PB, CH), F32),
    ("exth", (3 * PB, CH), F32), ("uf", (PB, FW), F32), ("su", (SEQS, PB, FW), F32),
    ("gf", (SEQS, PB, FW), BF), ("gg", (SEQS, 2, PB, HW), BF),
    ("ct", (SEQS, 2, PB, CH), BF), ("dux", (SEQS, PB, FW), BF), ("dup", (SEQS, PB, FW), BF),
    ("duo", (SEQS, PB, FW), BF), ("extd", (3 * PB, FW), F32), ("dwin", (SEQS, PB, 3 * FW), BF),
    ("dw", (SEQS, 2, PB, 3 * HW), BF), ("dnx", (SEQS, PB, CH), BF),
    ("hT", (NY, HW, 2 * SEQS * PB), BF), ("cT", (NY, HW, 2 * SEQS * PB), BF),
)
SEMS = (
    ("s_x", (SEQS,)), ("s_w", (2,)), ("s_top", (SEQS,)), ("s_out", (SEQS,)),
    ("hp_s", (SEQS,)), ("hp_r", (SEQS,)), ("ho_s", (SEQS,)), ("ho_r", (SEQS,)),
    ("g_s", (SEQS,)), ("g_r", (SEQS,)), ("c_s", (SEQS, NQ)), ("c_r", (SEQS, NQ)),
    ("dp_s", (SEQS,)), ("dp_r", (SEQS,)), ("do_s", (SEQS,)), ("do_r", (SEQS,)),
    ("dw_s", (SEQS, 3)), ("dw_r", (SEQS, 3)), ("hop_s", (SEQS, NQ)), ("hop_r", (SEQS, NQ)),
)


def step_kernel(scale, x_hbm, top_hbm, wc_hbm, wo_hbm, din_hbm, conv_ref, out_ref, *refs):
    r = dict(zip([n[0] for n in NAMES] + [n[0] for n in SEMS], refs))
    ring_refs = refs[len(NAMES) + len(SEMS):]
    xv, wc, wo, hx, ho, gx, exth, uf, su = (r[k] for k in ("xv", "wc", "wo", "hx", "ho", "gx", "exth", "uf", "su"))
    gf, gg, ct, dux, dup, duo, extd = (r[k] for k in ("gf", "gg", "ct", "dux", "dup", "duo", "extd"))
    dwin, dw, dnx, hT, cT = (r[k] for k in ("dwin", "dw", "dnx", "hT", "cT"))
    y, z, c = seq_place()
    s = lax.axis_index("section")
    j = seq_at(y, z, c)
    d = lax.shift_left(jnp.int32(DMAX // 2 ** (NS - 1)), s)
    partner = {"seq": seq_at(y, z, 1 - c)}
    outer_at = lax.rem(j + 2 * NY * NZ + 2 * c - 1, 2 * NY * NZ)
    outer = {"seq": outer_at}
    edge = jnp.logical_or(jnp.logical_and(c == 0, j == 0), jnp.logical_and(c == 1, j == 2 * NY * NZ - 1))
    barrier = pltpu.get_barrier_semaphore()
    for to in (partner, outer,
               {"seq": seq_at(y, lax.rem(z + NZ - 1, NZ), c)}, {"seq": seq_at(y, lax.rem(z + 1, NZ), c)},
               {"seq": seq_at(lax.rem(y + NY - 1, NY), z, c)}, {"seq": seq_at(lax.rem(y + 1, NY), z, c)},
               {"section": lax.rem(s + NS - 1, NS)}, {"section": lax.rem(s + 1, NS)}):
        pl.semaphore_signal(barrier, inc=1, device_id=to, device_id_type=pl.DeviceIdType.MESH)

    def mine(t):
        return pl.ds(pl.multiple_of(t * FW + c * HW, 128), HW)

    def theirs(t):
        return pl.ds(pl.multiple_of(t * FW + (1 - c) * HW, 128), HW)

    def part(q):
        return slice(q * QW, (q + 1) * QW)

    load_x = lambda b: pltpu.make_async_copy(x_hbm.at[0, b], xv.at[b], r["s_x"].at[b])
    load_wc = pltpu.make_async_copy(wc_hbm.at[0], wc, r["s_w"].at[0])
    load_wo = pltpu.make_async_copy(wo_hbm.at[0], wo, r["s_w"].at[1])
    load_top = lambda b: pltpu.make_async_copy(top_hbm.at[b], ct.at[b, 0], r["s_top"].at[b])
    save = lambda b: pltpu.make_async_copy(dnx.at[b], din_hbm.at[0, b], r["s_out"].at[b])
    h_near = lambda b: remote(hx.at[b, 0], hx.at[b, 1], r["hp_s"].at[b], r["hp_r"].at[b], partner)
    h_far = lambda b: remote(hx.at[b, 0], ho.at[b], r["ho_s"].at[b], r["ho_r"].at[b], outer)
    g_near = lambda b: remote(gf.at[b, :, theirs(0)], gg.at[b, 1], r["g_s"].at[b], r["g_r"].at[b], partner)
    c_near = lambda b, q: remote(ct.at[b, 0, :, part(q)], ct.at[b, 1, :, part(q)], r["c_s"].at[b, q], r["c_r"].at[b, q], partner)
    d_near = lambda b: remote(dux.at[b], dup.at[b], r["dp_s"].at[b], r["dp_r"].at[b], partner)
    d_far = lambda b: remote(dux.at[b], duo.at[b], r["do_s"].at[b], r["do_r"].at[b], outer)
    w_near = lambda b, t: remote(dwin.at[b, :, theirs(t)], dw.at[b, 1, :, pl.ds(t * HW, HW)], r["dw_s"].at[b, t], r["dw_r"].at[b, t], partner)
    hop = lambda b, q: remote(dnx.at[b, :, part(q)], ct.at[b, 0, :, part(q)], r["hop_s"].at[b, q], r["hop_r"].at[b, q],
                              {"section": lax.max(s - 1, 0)})

    for b in range(SEQS):
        load_x(b).start()
    load_wc.start()

    @pl.when(s == NS - 1)
    def _():
        for b in range(SEQS):
            load_top(b).start()

    load_wo.start()

    def forward_in(b):
        load_x(b).wait()

        def rows(i):
            at = pl.ds(pl.multiple_of(i * 16, 16), 16)
            for n in range(2):
                cols = slice(n * FW, (n + 1) * FW)
                h, slope = gelu_parts(xv[b, at, cols].astype(F32))
                hx[b, 0, at, cols] = h.astype(BF)
                gx[b, at, cols] = slope

        loop(PB // 16, rows)

        @pl.when(b == 0)
        def _():
            pl.semaphore_wait(barrier, 8)

        h_far(b).start()
        h_near(b).start()

    loop(SEQS, forward_in)
    load_wc.wait()
    load_wo.wait()
    own_at = pl.ds(PB, PB)
    near_at = pl.ds(pl.multiple_of((1 - c) * 2 * PB, PB), PB)
    far_at = pl.ds(pl.multiple_of(c * 2 * PB, PB), PB)

    def forward_mid(b):
        h_near(b).wait_recv()
        h_far(b).wait_recv()
        exth[own_at] = hx[b, 0].astype(F32)
        exth[near_at] = hx[b, 1].astype(F32)
        exth[far_at] = jnp.where(edge, 0.0, ho[b].astype(F32))
        acc = None
        for t in range(3):
            at = pl.ds(pl.multiple_of(PB + (t - 1) * d, 8), PB)
            got = jnp.dot(exth[at].astype(BF), wc[:, t * FW:(t + 1) * FW], preferred_element_type=F32)
            acc = got if acc is None else acc + got
        uf[...] = acc

        def rows(i):
            at = pl.ds(pl.multiple_of(i * 16, 16), 16)
            g, slope = gelu_parts(uf[at])
            gf[b, at] = g.astype(BF)
            su[b, at] = slope

        loop(PB // 16, rows)
        gg[b, 0] = gf[b, :, mine(0)]
        g_near(b).start()

    def turn(src, dst, b):
        at = pl.ds(pl.multiple_of(b * 2 * PB, 2 * PB), 2 * PB)
        for m in range(NY):
            dst[m, :, at] = src[b, :, :, m * HW:(m + 1) * HW].reshape(2 * PB, HW).T

    @pl.when(s < NS - 1)
    def _():
        loop(SEQS, forward_mid)
        loop(SEQS, lambda b: turn(hx, hT, b))

    def backward(b):
        @pl.when(s == NS - 1)
        def _():
            forward_mid(b)
            load_top(b).wait()

        dg = None
        for q in range(NQ):
            @pl.when(s < NS - 1)
            def _():
                hop(b, q).wait_recv()

            c_near(b, q).start()
            got = jnp.dot(ct[b, 0, :, part(q)], wo[q * QW:(q + 1) * QW], preferred_element_type=F32)
            dg = got if dg is None else dg + got
        du = (dg * su[b]).astype(BF)
        dux[b] = du
        d_far(b).start()
        d_near(b).start()
        extd[own_at] = du.astype(F32)
        d_near(b).wait_recv()
        extd[near_at] = dup[b].astype(F32)
        d_far(b).wait_recv()
        extd[far_at] = jnp.where(edge, 0.0, duo[b].astype(F32))
        for t in range(3):
            at = pl.ds(pl.multiple_of(PB - (t - 1) * d, 8), PB)
            dwin[b, :, t * FW:(t + 1) * FW] = extd[at].astype(BF)
        for q in range(NQ):
            dh = lax.dot_general(dwin[b], wc[q * QW:(q + 1) * QW], (((1,), (1,)), ((), ())), preferred_element_type=F32)
            dnx[b, :, part(q)] = (ct[b, 0, :, part(q)].astype(F32) + dh * gx[b, :, part(q)]).astype(BF)

            @pl.when(s > 0)
            def _():
                hop(b, q).start()

        save(b).start()
        for t in range(3):
            w_near(b, t).start()
            dw[b, 0, :, t * HW:(t + 1) * HW] = dwin[b, :, mine(t)]
        for q in range(NQ):
            c_near(b, q).wait_recv()
        turn(ct, cT, b)

    loop(SEQS, backward)

    @pl.when(s == NS - 1)
    def _():
        loop(SEQS, lambda b: turn(hx, hT, b))

    def gathered(b):
        for t in range(3):
            w_near(b, t).wait_recv()
        g_near(b).wait_recv()

    loop(SEQS, gathered)

    def fill(b, block):
        lhs = cT if b == 3 else hT
        for m in range(NY):
            rhs = gg[...] if b == 3 else dw[:, :, :, b * HW:(b + 1) * HW]
            got = jnp.dot(lhs[m], rhs.reshape(2 * SEQS * PB, HW), preferred_element_type=F32)
            block[m] = got.reshape(NZ, RB, HW)

    rs_run(fill, scale, conv_ref, out_ref, ring_refs)

    def ended(b):
        save(b).wait()
        h_near(b).wait_send()
        h_far(b).wait_send()
        g_near(b).wait_send()
        d_near(b).wait_send()
        d_far(b).wait_send()
        for t in range(3):
            w_near(b, t).wait_send()
        for q in range(NQ):
            c_near(b, q).wait_send()

            @pl.when(s > 0)
            def _():
                hop(b, q).wait_send()

    loop(SEQS, ended)


def body(layer_input, grad_top, w_conv, w_out):
    scale = 1.0 / math.sqrt(SEQS * PB * 2 * NY * NZ)
    scratch = [pltpu.VMEM(shape, kind) for _, shape, kind in NAMES]
    scratch += [pltpu.SemaphoreType.DMA(shape) for _, shape in SEMS]
    scratch += rs_scratch()
    dinput, conv_grad, out_grad = pl.pallas_call(
        functools.partial(step_kernel, scale),
        out_shape=(
            jax.ShapeDtypeStruct((1, SEQS, PB, CH), BF),
            jax.ShapeDtypeStruct((CH // (2 * NY * NZ), 3 * FW), F32),
            jax.ShapeDtypeStruct((CH // (2 * NY * NZ), FW), F32),
        ),
        in_specs=[pl.BlockSpec(memory_space=pl.ANY)] * 4,
        out_specs=(
            pl.BlockSpec(memory_space=pl.ANY),
            pl.BlockSpec(memory_space=pltpu.VMEM),
            pl.BlockSpec(memory_space=pltpu.VMEM),
        ),
        scratch_shapes=scratch,
        compiler_params=pltpu.CompilerParams(collective_id=1, has_side_effects=True, vmem_limit_bytes=63 << 20),
    )(layer_input, grad_top, w_conv, w_out)
    return (dinput, conv_grad[None], out_grad[None])


def solution(mesh):
    return jax.shard_map(
        body,
        mesh=mesh,
        in_specs=(
            P("section", None, "seq", None),
            P(None, "seq", None),
            P("section", None, None),
            P("section", None, None),
        ),
        out_specs=(
            P("section", None, "seq", None),
            P("section", "seq", None),
            P("section", "seq", None),
        ),
        check_vma=False,
    )
```

```python
import functools
import math

import jax
import jax.numpy as jnp
from jax import lax
from jax.experimental import pallas as pl
from jax.experimental.pallas import tpu as pltpu
from jax.sharding import PartitionSpec as P

BF = jnp.bfloat16
F32 = jnp.float32
NY, NZ = 4, 8
RB = 48
HW = 384


def seq_place():
    j = lax.axis_index("seq")
    c = lax.rem(j, 2)
    z = lax.rem(lax.div(j, 2), NZ)
    y = lax.div(j, 2 * NZ)
    return y, z, c


def seq_at(y, z, c):
    return (y * NZ + z) * 2 + c


SEQS = 4
PB = 64
CH = 1536
FW = 768
DMAX = 64
NS = 4
NQ = 3
QW = CH // NQ


def ring_bufs(n, nb, wd):
    hn = n // 2
    wu = HW - wd
    out = []
    for _ in range(2):
        out += [
            pltpu.VMEM((nb, RB, wd), BF),
            pltpu.VMEM((nb, RB, wu), BF),
            pltpu.VMEM((hn - 1, nb, RB, HW), BF),
            pltpu.VMEM((hn - 1, nb, RB, HW), BF),
        ]
    return out


class Ring:
    def __init__(self, n, nb, wd, me, down, up, index, block, refs, sems, first):
        self.n, self.nb, self.wd, self.me = n, nb, wd, me
        self.down, self.up, self.index, self.block = down, up, index, block
        self.s0d, self.s0u, self.sd, self.su, self.r0d, self.r0u, self.rd, self.ru = refs
        self.send, self.recv = sems
        self.first = first
        self.copies = []
        self.last = None

    def copy(self, src, dst, to):
        k = self.first + len(self.copies)
        one = pltpu.make_async_remote_copy(
            src_ref=src, dst_ref=dst, send_sem=self.send.at[k], recv_sem=self.recv.at[k],
            device_id={"seq": to}, device_id_type=pl.DeviceIdType.MESH)
        one.start()
        self.copies.append(one)
        return one

    def each(self, body):
        if self.nb == 1:
            body(0)
        else:
            lax.fori_loop(0, self.nb, lambda k, t: (body(k), t)[1], 0)

    def start(self):
        dest = lax.rem(self.me + self.n // 2, self.n)
        wd = self.wd

        def body(k):
            own = self.block[self.index(k, dest)]
            self.s0d[k] = own[:, :wd].astype(BF)
            self.s0u[k] = own[:, wd:].astype(BF)

        self.each(body)
        self.last = (self.copy(self.s0d, self.r0d, self.down), self.copy(self.s0u, self.r0u, self.up))

    def step(self, i):
        away = self.n // 2 - i
        wd = self.wd
        dest_d = lax.rem(self.me + self.n - away, self.n)
        dest_u = lax.rem(self.me + away, self.n)
        prev_d, prev_u = self.last
        prev_d.wait_recv()

        def body_d(k):
            own = self.block[self.index(k, dest_d)]
            if i == 1:
                self.sd[i - 1, k, :, :wd] = (own[:, :wd] + self.r0d[k].astype(F32)).astype(BF)
                self.sd[i - 1, k, :, wd:] = own[:, wd:].astype(BF)
            else:
                self.sd[i - 1, k] = (own + self.rd[i - 2, k].astype(F32)).astype(BF)

        self.each(body_d)
        new_d = self.copy(self.sd.at[i - 1], self.rd.at[i - 1], self.down)
        prev_u.wait_recv()

        def body_u(k):
            own = self.block[self.index(k, dest_u)]
            if i == 1:
                self.su[i - 1, k, :, :wd] = own[:, :wd].astype(BF)
                self.su[i - 1, k, :, wd:] = (own[:, wd:] + self.r0u[k].astype(F32)).astype(BF)
            else:
                self.su[i - 1, k] = (own + self.ru[i - 2, k].astype(F32)).astype(BF)

        self.each(body_u)
        new_u = self.copy(self.su.at[i - 1], self.ru.at[i - 1], self.up)
        self.last = (new_d, new_u)

    def finish(self):
        end = self.n // 2 - 2
        for one in self.last:
            one.wait_recv()

        def body(k):
            at = self.index(k, self.me)
            self.block[at] = self.block[at] + (self.rd[end, k].astype(F32) + self.ru[end, k].astype(F32))

        self.each(body)

    def drain(self):
        for one in self.copies:
            one.wait_send()


ORDERS = ("zy", "zy", "yz", "yz")
SPLITS = (256, 128, 256, 128)
ISSUE = (
    (2, 0), (0, 0), (1, 0), (3, 0), (0, 1), (2, 1), (1, 1), (3, 1), (0, 2), (1, 2), (2, 2), (0, 3), (1, 3), (2, 3),
    (3, 2), (0, 4), (0, 5), (1, 4), (2, 4), (3, 3), (0, 6), (1, 5), (2, 5), (3, 4), (1, 6), (2, 6), (3, 5), (3, 6),
)


def rs_scratch():
    shapes = [pltpu.VMEM((NY, NZ, RB, HW), F32) for _ in range(4)]
    for order, wd in zip(ORDERS, SPLITS):
        if order == "zy":
            shapes += ring_bufs(NZ, NY, wd) + ring_bufs(NY, 1, wd)
        else:
            shapes += ring_bufs(NY, NZ, wd) + ring_bufs(NZ, 1, wd)
    shapes += [
        pltpu.VMEM((4, RB // 2, HW), F32),
        pltpu.VMEM((4, RB // 2, HW), F32),
        pltpu.SemaphoreType.DMA((49,)),
        pltpu.SemaphoreType.DMA((49,)),
    ]
    return shapes


def rs_run(fill, scale, conv_ref, out_ref, refs):
    y, z, c = seq_place()
    blocks = refs[:4]
    bufs = refs[4:4 + 64]
    xs, xr, send, recv = refs[68:72]
    zd, zu = seq_at(y, lax.rem(z + NZ - 1, NZ), c), seq_at(y, lax.rem(z + 1, NZ), c)
    yd, yu = seq_at(lax.rem(y + NY - 1, NY), z, c), seq_at(lax.rem(y + 1, NY), z, c)
    plans = []
    first = 0
    for b in range(4):
        block = blocks[b]
        one, two = bufs[16 * b:16 * b + 8], bufs[16 * b + 8:16 * b + 16]
        wd = SPLITS[b]
        if ORDERS[b] == "zy":
            r1 = Ring(NZ, NY, wd, z, zd, zu, lambda k, d: (k, d), block, one, (send, recv), first)
            r2 = Ring(NY, 1, wd, y, yd, yu, lambda k, d: (d, z), block, two, (send, recv), first + 8)
            plan = [functools.partial(r1.step, i) for i in (1, 2, 3)]
            plan += [lambda r1=r1, r2=r2: (r1.finish(), r2.start()), functools.partial(r2.step, 1), r2.finish]
        else:
            r1 = Ring(NY, NZ, wd, y, yd, yu, lambda k, d: (d, k), block, one, (send, recv), first)
            r2 = Ring(NZ, 1, wd, z, zd, zu, lambda k, d: (y, d), block, two, (send, recv), first + 4)
            plan = [functools.partial(r1.step, 1), lambda r1=r1, r2=r2: (r1.finish(), r2.start())]
            plan += [functools.partial(r2.step, i) for i in (1, 2, 3)] + [r2.finish]
        first += 12
        plans.append((r1, r2, plan))
    for b, k in ISSUE:
        if k == 0:
            fill(b, blocks[b])
            plans[b][0].start()
        else:
            plans[b][2][k - 1]()
    half = RB // 2
    for b in range(4):
        xs[b] = blocks[b][y, z, pl.ds(pl.multiple_of((1 - c) * half, 8), half), :]
    swap = pltpu.make_async_remote_copy(
        src_ref=xs, dst_ref=xr, send_sem=send.at[48], recv_sem=recv.at[48],
        device_id={"seq": seq_at(y, z, 1 - c)}, device_id_type=pl.DeviceIdType.MESH)
    swap.start()

    def put(b, core, value):
        at = pl.multiple_of(core * HW, 128)
        if b == 3:
            out_ref[:, pl.ds(at, HW)] = value * scale
        else:
            conv_ref[:, pl.ds(pl.multiple_of(b * 2 * HW + at, 128), HW)] = value * scale

    for b in range(4):
        put(b, c, blocks[b][y, z, pl.ds(pl.multiple_of(c * half, 8), half), :])
    swap.wait_recv()
    for b in range(4):
        put(b, 1 - c, xr[b])
    swap.wait_send()
    for r1, r2, _ in plans:
        r1.drain()
        r2.drain()


def remote(src, dst, send, recv, to):
    return pltpu.make_async_remote_copy(
        src_ref=src, dst_ref=dst, send_sem=send, recv_sem=recv,
        device_id=to, device_id_type=pl.DeviceIdType.MESH)


def gelu_parts(v):
    cdf = 0.5 * (1.0 + lax.erf(v * 0.7071067811865476))
    return v * cdf, cdf + v * jnp.exp(-0.5 * v * v) * 0.3989422804014327


def loop(n, body):
    lax.fori_loop(0, n, lambda i, t: (body(i), t)[1], 0)


NAMES = (
    ("xv", (SEQS, PB, CH), BF), ("wc", (CH, 3 * FW), BF), ("wt", (3 * FW, CH), BF), ("wo", (CH, FW), BF),
    ("hx", (SEQS, 2, PB, CH), BF), ("ho", (SEQS, PB, CH), BF), ("gx", (SEQS, PB, CH), F32),
    ("exth", (3 * PB, CH), F32), ("uf", (PB, FW), F32), ("su", (SEQS, PB, FW), F32),
    ("gf", (SEQS, PB, FW), BF), ("gg", (SEQS, 2, PB, HW), BF),
    ("ct", (SEQS, 2, PB, CH), BF), ("dux", (SEQS, PB, FW), BF), ("dup", (SEQS, PB, FW), BF),
    ("duo", (SEQS, PB, FW), BF), ("extd", (3 * PB, FW), F32), ("dwin", (SEQS, PB, 3 * FW), BF),
    ("dw", (SEQS, 2, PB, 3 * HW), BF), ("dnx", (SEQS, PB, CH), BF),
    ("hT", (NY, HW, 2 * SEQS * PB), BF), ("cT", (NY, HW, 2 * SEQS * PB), BF),
)
SEMS = (
    ("s_x", (SEQS,)), ("s_w", (2,)), ("s_top", (SEQS,)), ("s_out", (SEQS,)),
    ("hp_s", (SEQS,)), ("hp_r", (SEQS,)), ("ho_s", (SEQS,)), ("ho_r", (SEQS,)),
    ("g_s", (SEQS,)), ("g_r", (SEQS,)), ("c_s", (SEQS, NQ)), ("c_r", (SEQS, NQ)),
    ("dp_s", (SEQS,)), ("dp_r", (SEQS,)), ("do_s", (SEQS,)), ("do_r", (SEQS,)),
    ("dw_s", (SEQS, 3)), ("dw_r", (SEQS, 3)), ("hop_s", (SEQS, NQ)), ("hop_r", (SEQS, NQ)),
)


def step_kernel(scale, x_hbm, top_hbm, wc_hbm, wo_hbm, din_hbm, conv_ref, out_ref, *refs):
    r = dict(zip([n[0] for n in NAMES] + [n[0] for n in SEMS], refs))
    ring_refs = refs[len(NAMES) + len(SEMS):]
    wt = r["wt"]
    xv, wc, wo, hx, ho, gx, exth, uf, su = (r[k] for k in ("xv", "wc", "wo", "hx", "ho", "gx", "exth", "uf", "su"))
    gf, gg, ct, dux, dup, duo, extd = (r[k] for k in ("gf", "gg", "ct", "dux", "dup", "duo", "extd"))
    dwin, dw, dnx, hT, cT = (r[k] for k in ("dwin", "dw", "dnx", "hT", "cT"))
    y, z, c = seq_place()
    s = lax.axis_index("section")
    j = seq_at(y, z, c)
    d = lax.shift_left(jnp.int32(DMAX // 2 ** (NS - 1)), s)
    partner = {"seq": seq_at(y, z, 1 - c)}
    outer_at = lax.rem(j + 2 * NY * NZ + 2 * c - 1, 2 * NY * NZ)
    outer = {"seq": outer_at}
    edge = jnp.logical_or(jnp.logical_and(c == 0, j == 0), jnp.logical_and(c == 1, j == 2 * NY * NZ - 1))
    barrier = pltpu.get_barrier_semaphore()
    for to in (partner, outer,
               {"seq": seq_at(y, lax.rem(z + NZ - 1, NZ), c)}, {"seq": seq_at(y, lax.rem(z + 1, NZ), c)},
               {"seq": seq_at(lax.rem(y + NY - 1, NY), z, c)}, {"seq": seq_at(lax.rem(y + 1, NY), z, c)},
               {"section": lax.rem(s + NS - 1, NS)}, {"section": lax.rem(s + 1, NS)}):
        pl.semaphore_signal(barrier, inc=1, device_id=to, device_id_type=pl.DeviceIdType.MESH)

    def mine(t):
        return pl.ds(pl.multiple_of(t * FW + c * HW, 128), HW)

    def theirs(t):
        return pl.ds(pl.multiple_of(t * FW + (1 - c) * HW, 128), HW)

    def part(q):
        return slice(q * QW, (q + 1) * QW)

    load_x = lambda b: pltpu.make_async_copy(x_hbm.at[0, b], xv.at[b], r["s_x"].at[b])
    load_wc = pltpu.make_async_copy(wc_hbm.at[0], wc, r["s_w"].at[0])
    load_wo = pltpu.make_async_copy(wo_hbm.at[0], wo, r["s_w"].at[1])
    load_top = lambda b: pltpu.make_async_copy(top_hbm.at[b], ct.at[b, 0], r["s_top"].at[b])
    save = lambda b: pltpu.make_async_copy(dnx.at[b], din_hbm.at[0, b], r["s_out"].at[b])
    h_near = lambda b: remote(hx.at[b, 0], hx.at[b, 1], r["hp_s"].at[b], r["hp_r"].at[b], partner)
    h_far = lambda b: remote(hx.at[b, 0], ho.at[b], r["ho_s"].at[b], r["ho_r"].at[b], outer)
    g_near = lambda b: remote(gf.at[b, :, theirs(0)], gg.at[b, 1], r["g_s"].at[b], r["g_r"].at[b], partner)
    c_near = lambda b, q: remote(ct.at[b, 0, :, part(q)], ct.at[b, 1, :, part(q)], r["c_s"].at[b, q], r["c_r"].at[b, q], partner)
    d_near = lambda b: remote(dux.at[b], dup.at[b], r["dp_s"].at[b], r["dp_r"].at[b], partner)

    def d_far(b, act):
        for n, here in ((16, s < NS - 2), (32, s == NS - 2), (64, s == NS - 1)):
            at = pl.ds(pl.multiple_of(c * (PB - n), 16), n)

            @pl.when(here)
            def _():
                act(remote(dux.at[b, at], duo.at[b, at], r["do_s"].at[b], r["do_r"].at[b], outer))

    w_near = lambda b, t: remote(dwin.at[b, :, theirs(t)], dw.at[b, 1, :, pl.ds(t * HW, HW)], r["dw_s"].at[b, t], r["dw_r"].at[b, t], partner)
    hop = lambda b, q: remote(dnx.at[b, :, part(q)], ct.at[b, 0, :, part(q)], r["hop_s"].at[b, q], r["hop_r"].at[b, q],
                              {"section": lax.max(s - 1, 0)})

    for b in range(SEQS):
        load_x(b).start()
    load_wc.start()

    @pl.when(s == NS - 1)
    def _():
        for b in range(SEQS):
            load_top(b).start()

    load_wo.start()

    def forward_in(b):
        load_x(b).wait()

        def rows(i):
            at = pl.ds(pl.multiple_of(i * 16, 16), 16)
            for n in range(2):
                cols = slice(n * FW, (n + 1) * FW)
                h, slope = gelu_parts(xv[b, at, cols].astype(F32))
                hx[b, 0, at, cols] = h.astype(BF)
                gx[b, at, cols] = slope

        loop(PB // 16, rows)

        @pl.when(b == 0)
        def _():
            pl.semaphore_wait(barrier, 8)

        @pl.when(jnp.logical_or(s < NS - 1, b < 2))
        def _():
            h_far(b).start()

        h_near(b).start()

    loop(SEQS, forward_in)
    load_wc.wait()

    def flip(n):
        at = pl.ds(pl.multiple_of(n * 256, 256), 256)
        for m in range(CH // 256):
            wt[at, m * 256:(m + 1) * 256] = wc[m * 256:(m + 1) * 256, at].T

    loop(3 * FW // 256, flip)
    load_wo.wait()
    own_at = pl.ds(PB, PB)
    near_at = pl.ds(pl.multiple_of((1 - c) * 2 * PB, PB), PB)
    far_at = pl.ds(pl.multiple_of(c * 2 * PB, PB), PB)

    def forward_mid(b):
        h_near(b).wait_recv()
        h_far(b).wait_recv()
        exth[own_at] = hx[b, 0].astype(F32)
        exth[near_at] = hx[b, 1].astype(F32)
        exth[far_at] = jnp.where(edge, 0.0, ho[b].astype(F32))
        acc = None
        for t in range(3):
            at = pl.ds(pl.multiple_of(PB + (t - 1) * d, 8), PB)
            got = jnp.dot(exth[at].astype(BF), wc[:, t * FW:(t + 1) * FW], preferred_element_type=F32)
            acc = got if acc is None else acc + got
        uf[...] = acc

        def rows(i):
            at = pl.ds(pl.multiple_of(i * 16, 16), 16)
            g, slope = gelu_parts(uf[at])
            gf[b, at] = g.astype(BF)
            su[b, at] = slope

        loop(PB // 16, rows)
        gg[b, 0] = gf[b, :, mine(0)]
        g_near(b).start()

    def turn(src, dst, b):
        at = pl.ds(pl.multiple_of(b * 2 * PB, 2 * PB), 2 * PB)
        for m in range(NY):
            dst[m, :, at] = src[b, :, :, m * HW:(m + 1) * HW].reshape(2 * PB, HW).T

    @pl.when(s < NS - 1)
    def _():
        loop(SEQS, forward_mid)
        loop(SEQS, lambda b: turn(hx, hT, b))

    def front(b):
        dg = None
        for q in range(NQ):
            @pl.when(s < NS - 1)
            def _():
                hop(b, q).wait_recv()

            got = jnp.dot(ct[b, 0, :, part(q)], wo[q * QW:(q + 1) * QW], preferred_element_type=F32)
            dg = got if dg is None else dg + got
        dux[b] = (dg * su[b]).astype(BF)
        d_far(b, lambda one: one.start())
        d_near(b).start()
        for q in range(NQ):
            c_near(b, q).start()

    def first_front(b):
        forward_mid(b)
        load_top(b).wait()
        front(b)

        @pl.when(b < SEQS - 2)
        def _():
            h_far(b + 2).start()

    @pl.when(s == NS - 1)
    def _():
        first_front(0)

    def backward(b):
        @pl.when(s < NS - 1)
        def _():
            front(b)

        @pl.when(jnp.logical_and(s == NS - 1, b < SEQS - 1))
        def _():
            first_front(b + 1)

        extd[own_at] = dux[b].astype(F32)
        d_near(b).wait_recv()
        extd[near_at] = dup[b].astype(F32)
        d_far(b, lambda one: one.wait_recv())
        extd[far_at] = jnp.where(edge, 0.0, duo[b].astype(F32))
        for t in range(3):
            at = pl.ds(pl.multiple_of(PB - (t - 1) * d, 8), PB)
            dwin[b, :, t * FW:(t + 1) * FW] = extd[at].astype(BF)
        for q in range(NQ):
            dh = jnp.dot(dwin[b], wt[:, part(q)], preferred_element_type=F32)
            dnx[b, :, part(q)] = (ct[b, 0, :, part(q)].astype(F32) + dh * gx[b, :, part(q)]).astype(BF)

            @pl.when(s > 0)
            def _():
                hop(b, q).start()

        save(b).start()
        for t in range(3):
            w_near(b, t).start()
            dw[b, 0, :, t * HW:(t + 1) * HW] = dwin[b, :, mine(t)]
        for q in range(NQ):
            c_near(b, q).wait_recv()
        turn(ct, cT, b)

    loop(SEQS, backward)

    @pl.when(s == NS - 1)
    def _():
        loop(SEQS, lambda b: turn(hx, hT, b))

    def gathered(b):
        for t in range(3):
            w_near(b, t).wait_recv()
        g_near(b).wait_recv()

    loop(SEQS, gathered)

    def fill(b, block):
        lhs = cT if b == 3 else hT
        for m in range(NY):
            rhs = gg[...] if b == 3 else dw[:, :, :, b * HW:(b + 1) * HW]
            got = jnp.dot(lhs[m], rhs.reshape(2 * SEQS * PB, HW), preferred_element_type=F32)
            block[m] = got.reshape(NZ, RB, HW)

    rs_run(fill, scale, conv_ref, out_ref, ring_refs)

    def ended(b):
        save(b).wait()
        h_near(b).wait_send()
        h_far(b).wait_send()
        g_near(b).wait_send()
        d_near(b).wait_send()
        d_far(b, lambda one: one.wait_send())
        for t in range(3):
            w_near(b, t).wait_send()
        for q in range(NQ):
            c_near(b, q).wait_send()

            @pl.when(s > 0)
            def _():
                hop(b, q).wait_send()

    loop(SEQS, ended)


def pass_on(a, b, c, a_out, b_out, c_out):
    a_out[...] = a[...]
    b_out[...] = b[...]
    c_out[...] = c[...]


def body(layer_input, grad_top, w_conv, w_out):
    scale = 1.0 / math.sqrt(SEQS * PB * 2 * NY * NZ)
    scratch = [pltpu.VMEM(shape, kind) for _, shape, kind in NAMES]
    scratch += [pltpu.SemaphoreType.DMA(shape) for _, shape in SEMS]
    scratch += rs_scratch()
    dinput, conv_grad, out_grad = pl.pallas_call(
        functools.partial(step_kernel, scale),
        out_shape=(
            jax.ShapeDtypeStruct((1, SEQS, PB, CH), BF),
            jax.ShapeDtypeStruct((CH // (2 * NY * NZ), 3 * FW), F32),
            jax.ShapeDtypeStruct((CH // (2 * NY * NZ), FW), F32),
        ),
        in_specs=[pl.BlockSpec(memory_space=pl.ANY)] * 4,
        out_specs=(
            pl.BlockSpec(memory_space=pl.ANY),
            pl.BlockSpec(memory_space=pltpu.VMEM),
            pl.BlockSpec(memory_space=pltpu.VMEM),
        ),
        scratch_shapes=scratch,
        compiler_params=pltpu.CompilerParams(collective_id=1, has_side_effects=True, vmem_limit_bytes=63 << 20),
    )(layer_input, grad_top, w_conv, w_out)
    results = (dinput, conv_grad[None], out_grad[None])
    return pl.pallas_call(
        pass_on,
        out_shape=tuple(jax.ShapeDtypeStruct(one.shape, one.dtype) for one in results),
        in_specs=[pl.BlockSpec(memory_space=pltpu.VMEM)] * 3,
        out_specs=(pl.BlockSpec(memory_space=pltpu.VMEM),) * 3,
    )(*results)


def solution(mesh):
    return jax.shard_map(
        body,
        mesh=mesh,
        in_specs=(
            P("section", None, "seq", None),
            P(None, "seq", None),
            P("section", None, None),
            P("section", None, None),
        ),
        out_specs=(
            P("section", None, "seq", None),
            P("section", "seq", None),
            P("section", "seq", None),
        ),
        check_vma=False,
    )
```

```python
import functools
import math

import jax
import jax.numpy as jnp
from jax import lax
from jax.experimental import pallas as pl
from jax.experimental.pallas import tpu as pltpu
from jax.sharding import PartitionSpec as P

BF = jnp.bfloat16
F32 = jnp.float32
NY, NZ = 4, 8
RB = 48
HW = 384


def seq_place():
    j = lax.axis_index("seq")
    c = lax.rem(j, 2)
    z = lax.rem(lax.div(j, 2), NZ)
    y = lax.div(j, 2 * NZ)
    return y, z, c


def seq_at(y, z, c):
    return (y * NZ + z) * 2 + c


SEQS = 4
PB = 64
CH = 1536
FW = 768
DMAX = 64
NS = 4
NQ = 3
QW = CH // NQ


def ring_bufs(n, nb, wd):
    hn = n // 2
    wu = HW - wd
    out = []
    for _ in range(2):
        out += [
            pltpu.VMEM((nb, RB, wd), BF),
            pltpu.VMEM((nb, RB, wu), BF),
            pltpu.VMEM((hn - 1, nb, RB, HW), BF),
            pltpu.VMEM((hn - 1, nb, RB, HW), BF),
        ]
    return out


class Ring:
    def __init__(self, n, nb, wd, me, down, up, index, block, refs, sems, first):
        self.n, self.nb, self.wd, self.me = n, nb, wd, me
        self.down, self.up, self.index, self.block = down, up, index, block
        self.s0d, self.s0u, self.sd, self.su, self.r0d, self.r0u, self.rd, self.ru = refs
        self.send, self.recv = sems
        self.first = first
        self.copies = []
        self.last = None

    def copy(self, ends, to):
        k = self.first + len(self.copies)

        def make():
            src, dst = ends()
            return remote(src, dst, self.send.at[k], self.recv.at[k], {"seq": to})

        make().start()
        self.copies.append(make)
        return make

    def each(self, body):
        if self.nb == 1:
            body(0)
        else:
            lax.fori_loop(0, self.nb, lambda k, t: (body(k), t)[1], 0)

    def start(self):
        dest = lax.rem(self.me + self.n // 2, self.n)
        wd = self.wd

        def body(k):
            own = self.block[self.index(k, dest)]
            self.s0d[k] = own[:, :wd].astype(BF)
            self.s0u[k] = own[:, wd:].astype(BF)

        self.each(body)
        self.last = (self.copy(lambda: (self.s0d, self.r0d), self.down), self.copy(lambda: (self.s0u, self.r0u), self.up))

    def step(self, i):
        away = self.n // 2 - i
        wd = self.wd
        dest_d = lax.rem(self.me + self.n - away, self.n)
        dest_u = lax.rem(self.me + away, self.n)
        prev_d, prev_u = self.last
        prev_d().wait_recv()

        def body_d(k):
            own = self.block[self.index(k, dest_d)]
            if i == 1:
                self.sd[i - 1, k, :, :wd] = (own[:, :wd] + self.r0d[k].astype(F32)).astype(BF)
                self.sd[i - 1, k, :, wd:] = own[:, wd:].astype(BF)
            else:
                self.sd[i - 1, k] = (own + self.rd[i - 2, k].astype(F32)).astype(BF)

        self.each(body_d)
        new_d = self.copy(lambda: (self.sd.at[i - 1], self.rd.at[i - 1]), self.down)
        prev_u().wait_recv()

        def body_u(k):
            own = self.block[self.index(k, dest_u)]
            if i == 1:
                self.su[i - 1, k, :, :wd] = own[:, :wd].astype(BF)
                self.su[i - 1, k, :, wd:] = (own[:, wd:] + self.r0u[k].astype(F32)).astype(BF)
            else:
                self.su[i - 1, k] = (own + self.ru[i - 2, k].astype(F32)).astype(BF)

        self.each(body_u)
        new_u = self.copy(lambda: (self.su.at[i - 1], self.ru.at[i - 1]), self.up)
        self.last = (new_d, new_u)

    def finish(self):
        end = self.n // 2 - 2
        for one in self.last:
            one().wait_recv()

        def body(k):
            at = self.index(k, self.me)
            self.block[at] = self.block[at] + (self.rd[end, k].astype(F32) + self.ru[end, k].astype(F32))

        self.each(body)

    def drain(self):
        for one in self.copies:
            one().wait_send()


ORDERS = ("zy", "yz", "yz", "zy", "yz")
SPLITS = (256, 256, 128, 128, 256)
NB = 5
ISSUE = (
    (1, 0), (0, 0), (3, 0), (2, 0), (4, 0), (0, 1), (1, 1), (3, 1), (2, 1), (4, 1), (0, 2), (3, 2),
    (1, 2), (0, 3), (3, 3), (1, 3), (2, 2), (4, 2), (0, 4), (0, 5), (3, 4), (1, 4), (2, 3), (4, 3),
    (0, 6), (3, 5), (1, 5), (2, 4), (4, 4), (3, 6), (1, 6), (2, 5), (4, 5), (2, 6), (4, 6),
)


def rs_scratch():
    shapes = [pltpu.VMEM((NY, NZ, RB, HW), F32) for _ in range(NB)]
    for order, wd in zip(ORDERS, SPLITS):
        if order == "zy":
            shapes += ring_bufs(NZ, NY, wd) + ring_bufs(NY, 1, wd)
        else:
            shapes += ring_bufs(NY, NZ, wd) + ring_bufs(NZ, 1, wd)
    shapes += [
        pltpu.VMEM((NB, RB // 2, HW), F32),
        pltpu.VMEM((NB, RB // 2, HW), F32),
        pltpu.VMEM((RB // 2, 2 * HW), F32),
        pltpu.VMEM((RB // 2, 2 * HW), F32),
        pltpu.SemaphoreType.DMA((12 * NB + 4,)),
        pltpu.SemaphoreType.DMA((12 * NB + 4,)),
    ]
    return shapes


def rs_run(fill, beside, scale, conv_ref, out_ref, refs):
    y, z, c = seq_place()
    s = lax.axis_index("section")
    conds = (None, None, None, s > 0, s == NS - 1)

    def guarded(b, act):
        if conds[b] is None:
            act()
        else:
            pl.when(conds[b])(lambda: (act(), None)[1])

    blocks = refs[:NB]
    bufs = refs[NB:NB + 16 * NB]
    xs, xr, total, below, send, recv = refs[17 * NB:17 * NB + 6]
    zd, zu = seq_at(y, lax.rem(z + NZ - 1, NZ), c), seq_at(y, lax.rem(z + 1, NZ), c)
    yd, yu = seq_at(lax.rem(y + NY - 1, NY), z, c), seq_at(lax.rem(y + 1, NY), z, c)
    plans = []
    first = 0
    for b in range(NB):
        block = blocks[b]
        one, two = bufs[16 * b:16 * b + 8], bufs[16 * b + 8:16 * b + 16]
        wd = SPLITS[b]
        if ORDERS[b] == "zy":
            r1 = Ring(NZ, NY, wd, z, zd, zu, lambda k, d: (k, d), block, one, (send, recv), first)
            r2 = Ring(NY, 1, wd, y, yd, yu, lambda k, d: (d, z), block, two, (send, recv), first + 8)
            plan = [functools.partial(r1.step, i) for i in (1, 2, 3)]
            plan += [lambda r1=r1, r2=r2: (r1.finish(), r2.start()), functools.partial(r2.step, 1), r2.finish]
        else:
            r1 = Ring(NY, NZ, wd, y, yd, yu, lambda k, d: (d, k), block, one, (send, recv), first)
            r2 = Ring(NZ, 1, wd, z, zd, zu, lambda k, d: (y, d), block, two, (send, recv), first + 4)
            plan = [functools.partial(r1.step, 1), lambda r1=r1, r2=r2: (r1.finish(), r2.start())]
            plan += [functools.partial(r2.step, i) for i in (1, 2, 3)] + [r2.finish]
        first += 12
        plans.append((r1, r2, plan))
    for n, (b, k) in enumerate(ISSUE):
        if n == NB:
            beside()
        if k == 0:
            guarded(b, lambda b=b: (fill(b, blocks[b]), plans[b][0].start()))
        else:
            guarded(b, plans[b][2][k - 1])
    half = RB // 2
    partner = {"seq": seq_at(y, z, 1 - c)}
    conv_swap, low_swap, own_swap = (
        remote(xs.at[at], xr.at[at], send.at[12 * NB + n], recv.at[12 * NB + n], partner)
        for n, at in enumerate((pl.ds(0, 3), pl.ds(3, 1), pl.ds(4, 1))))
    lower = remote(total, below, send.at[12 * NB + 3], recv.at[12 * NB + 3], {"section": lax.max(s - 1, 0)})

    def rows(b, core):
        return blocks[b][y, z, pl.ds(pl.multiple_of(core * half, 8), half), :]

    def put(ref, at, core, value):
        ref[:, pl.ds(pl.multiple_of(at + core * HW, 128), HW)] = value * scale

    def swap(one, first, count):
        for b in range(first, first + count):
            xs[b] = rows(b, 1 - c)
        one.start()

    swap(conv_swap, 0, 3)
    guarded(3, lambda: swap(low_swap, 3, 1))
    guarded(4, lambda: swap(own_swap, 4, 1))

    def lower_out():
        put(total, 0, c, rows(3, c))
        low_swap.wait_recv()
        put(total, 0, 1 - c, xr[3])
        lower.start()

    guarded(3, lower_out)
    for b in range(3):
        put(conv_ref, b * 2 * HW, c, rows(b, c))
    conv_swap.wait_recv()
    for b in range(3):
        put(conv_ref, b * 2 * HW, 1 - c, xr[b])

    def own_out():
        put(out_ref, 0, c, rows(4, c))
        own_swap.wait_recv()
        put(out_ref, 0, 1 - c, xr[4])
        own_swap.wait_send()

    guarded(4, own_out)

    @pl.when(s < NS - 1)
    def _():
        lower.wait_recv()
        out_ref[...] = below[...]

    def lower_end():
        low_swap.wait_send()
        lower.wait_send()

    guarded(3, lower_end)
    conv_swap.wait_send()
    for b, (r1, r2, _) in enumerate(plans):
        guarded(b, lambda r1=r1, r2=r2: (r1.drain(), r2.drain()))


def remote(src, dst, send, recv, to):
    return pltpu.make_async_remote_copy(
        src_ref=src, dst_ref=dst, send_sem=send, recv_sem=recv,
        device_id=to, device_id_type=pl.DeviceIdType.MESH)


def gelu_parts(v):
    cdf = 0.5 * (1.0 + lax.erf(v * 0.7071067811865476))
    return v * cdf, cdf + v * jnp.exp(-0.5 * v * v) * 0.3989422804014327


def loop(n, body):
    lax.fori_loop(0, n, lambda i, t: (body(i), t)[1], 0)


NAMES = (
    ("xv", (SEQS, PB, CH), BF), ("wc", (CH, 3 * FW), BF), ("wt", (3 * FW, CH), BF), ("wo", (CH, FW), BF),
    ("hx", (SEQS, 2, PB, CH), BF), ("ho", (SEQS, PB, CH), BF), ("gx", (SEQS, PB, CH), F32),
    ("exth", (3 * PB, CH), F32), ("uf", (PB, FW), F32), ("su", (SEQS, PB, FW), F32),
    ("gf", (SEQS, PB, FW), BF), ("gg", (SEQS, 2, PB, HW), BF),
    ("ct", (SEQS, 2, PB, CH), BF), ("dux", (SEQS, PB, FW), BF), ("dup", (SEQS, PB, FW), BF),
    ("duo", (SEQS, PB, FW), BF), ("extd", (3 * PB, FW), F32), ("dwin", (SEQS, PB, 3 * FW), BF),
    ("dw", (SEQS, 2, PB, 3 * HW), BF), ("dnx", (SEQS, PB, CH), BF),
    ("hT", (NY, HW, 2 * SEQS * PB), BF), ("cT", (NY, HW, 2 * SEQS * PB), BF), ("tT", (NY, HW, 2 * SEQS * PB), BF),
    ("gu", (SEQS, 2, PB, HW), BF), ("nx", (SEQS, PB, CH), BF),
)
SEMS = (
    ("s_x", (SEQS,)), ("s_w", (2,)), ("s_top", (SEQS,)), ("s_out", (SEQS,)),
    ("hp_s", (SEQS,)), ("hp_r", (SEQS,)), ("ho_s", (SEQS,)), ("ho_r", (SEQS,)),
    ("g_s", (SEQS,)), ("g_r", (SEQS,)), ("c_s", (SEQS, NQ)), ("c_r", (SEQS, NQ)),
    ("dp_s", (SEQS,)), ("dp_r", (SEQS,)), ("do_s", (SEQS,)), ("do_r", (SEQS,)),
    ("dw_s", (SEQS, 3)), ("dw_r", (SEQS, 3)), ("hop_s", (SEQS, NQ)), ("hop_r", (SEQS, NQ)),
    ("n_s", (SEQS,)), ("n_r", (SEQS,)), ("u_s", (SEQS,)), ("u_r", (SEQS,)),
)


def step_kernel(scale, x_hbm, top_hbm, wc_hbm, wo_hbm, din_hbm, conv_ref, out_ref, *refs):
    r = dict(zip([n[0] for n in NAMES] + [n[0] for n in SEMS], refs))
    ring_refs = refs[len(NAMES) + len(SEMS):]
    wt = r["wt"]
    xv, wc, wo, hx, ho, gx, exth, uf, su = (r[k] for k in ("xv", "wc", "wo", "hx", "ho", "gx", "exth", "uf", "su"))
    gf, gg, ct, dux, dup, duo, extd = (r[k] for k in ("gf", "gg", "ct", "dux", "dup", "duo", "extd"))
    dwin, dw, dnx, hT, cT, tT, gu, nx = (r[k] for k in ("dwin", "dw", "dnx", "hT", "cT", "tT", "gu", "nx"))
    y, z, c = seq_place()
    s = lax.axis_index("section")
    j = seq_at(y, z, c)
    d = lax.shift_left(jnp.int32(DMAX // 2 ** (NS - 1)), s)
    partner = {"seq": seq_at(y, z, 1 - c)}
    outer_at = lax.rem(j + 2 * NY * NZ + 2 * c - 1, 2 * NY * NZ)
    outer = {"seq": outer_at}
    edge = jnp.logical_or(jnp.logical_and(c == 0, j == 0), jnp.logical_and(c == 1, j == 2 * NY * NZ - 1))
    barrier = pltpu.get_barrier_semaphore()
    for to in (partner, outer,
               {"seq": seq_at(y, lax.rem(z + NZ - 1, NZ), c)}, {"seq": seq_at(y, lax.rem(z + 1, NZ), c)},
               {"seq": seq_at(lax.rem(y + NY - 1, NY), z, c)}, {"seq": seq_at(lax.rem(y + 1, NY), z, c)},
               {"section": lax.rem(s + NS - 1, NS)}, {"section": lax.rem(s + 1, NS)}):
        pl.semaphore_signal(barrier, inc=1, device_id=to, device_id_type=pl.DeviceIdType.MESH)

    def mine(t):
        return pl.ds(pl.multiple_of(t * FW + c * HW, 128), HW)

    def theirs(t):
        return pl.ds(pl.multiple_of(t * FW + (1 - c) * HW, 128), HW)

    def part(q):
        return slice(q * QW, (q + 1) * QW)

    load_x = lambda b: pltpu.make_async_copy(x_hbm.at[0, b], xv.at[b], r["s_x"].at[b])
    load_wc = pltpu.make_async_copy(wc_hbm.at[0], wc, r["s_w"].at[0])
    load_wo = pltpu.make_async_copy(wo_hbm.at[0], wo, r["s_w"].at[1])
    load_top = lambda b: pltpu.make_async_copy(top_hbm.at[b], ct.at[b, 0], r["s_top"].at[b])
    save = lambda b: pltpu.make_async_copy(dnx.at[b], din_hbm.at[0, b], r["s_out"].at[b])
    h_near = lambda b: remote(hx.at[b, 0], hx.at[b, 1], r["hp_s"].at[b], r["hp_r"].at[b], partner)
    h_far = lambda b: remote(hx.at[b, 0], ho.at[b], r["ho_s"].at[b], r["ho_r"].at[b], outer)
    g_near = lambda b: remote(gf.at[b, :, theirs(0)], gg.at[b, 1], r["g_s"].at[b], r["g_r"].at[b], partner)
    c_near = lambda b, q: remote(ct.at[b, 0, :, part(q)], ct.at[b, 1, :, part(q)], r["c_s"].at[b, q], r["c_r"].at[b, q], partner)
    d_near = lambda b: remote(dux.at[b], dup.at[b], r["dp_s"].at[b], r["dp_r"].at[b], partner)

    def d_far(b, act):
        for n, here in ((16, s < NS - 2), (32, s == NS - 2), (64, s == NS - 1)):
            at = pl.ds(pl.multiple_of(c * (PB - n), 16), n)

            @pl.when(here)
            def _():
                act(remote(dux.at[b, at], duo.at[b, at], r["do_s"].at[b], r["do_r"].at[b], outer))

    n_near = lambda b: remote(dnx.at[b], nx.at[b], r["n_s"].at[b], r["n_r"].at[b], partner)
    g_up = lambda b: remote(gg.at[b], gu.at[b], r["u_s"].at[b], r["u_r"].at[b], {"section": lax.min(s + 1, NS - 1)})
    w_near = lambda b, t: remote(dwin.at[b, :, theirs(t)], dw.at[b, 1, :, pl.ds(t * HW, HW)], r["dw_s"].at[b, t], r["dw_r"].at[b, t], partner)
    hop = lambda b, q: remote(dnx.at[b, :, part(q)], ct.at[b, 0, :, part(q)], r["hop_s"].at[b, q], r["hop_r"].at[b, q],
                              {"section": lax.max(s - 1, 0)})

    for b in range(SEQS):
        load_x(b).start()
    load_wc.start()

    @pl.when(s == NS - 1)
    def _():
        for b in range(SEQS):
            load_top(b).start()

    load_wo.start()

    def forward_in(b):
        load_x(b).wait()

        def rows(i):
            at = pl.ds(pl.multiple_of(i * 16, 16), 16)
            for n in range(2):
                cols = slice(n * FW, (n + 1) * FW)
                h, slope = gelu_parts(xv[b, at, cols].astype(F32))
                hx[b, 0, at, cols] = h.astype(BF)
                gx[b, at, cols] = slope

        loop(PB // 16, rows)

        @pl.when(b == 0)
        def _():
            pl.semaphore_wait(barrier, 8)

        @pl.when(jnp.logical_or(s < NS - 1, b < 2))
        def _():
            h_far(b).start()

        h_near(b).start()

    loop(SEQS, forward_in)
    load_wc.wait()

    def flip(n):
        at = pl.ds(pl.multiple_of(n * 256, 256), 256)
        for m in range(CH // 256):
            wt[at, m * 256:(m + 1) * 256] = wc[m * 256:(m + 1) * 256, at].T

    loop(3 * FW // 256, flip)
    load_wo.wait()
    own_at = pl.ds(PB, PB)
    near_at = pl.ds(pl.multiple_of((1 - c) * 2 * PB, PB), PB)
    far_at = pl.ds(pl.multiple_of(c * 2 * PB, PB), PB)

    def forward_mid(b):
        h_near(b).wait_recv()
        h_far(b).wait_recv()
        exth[own_at] = hx[b, 0].astype(F32)
        exth[near_at] = hx[b, 1].astype(F32)
        exth[far_at] = jnp.where(edge, 0.0, ho[b].astype(F32))
        acc = None
        for t in range(3):
            at = pl.ds(pl.multiple_of(PB + (t - 1) * d, 8), PB)
            got = jnp.dot(exth[at].astype(BF), wc[:, t * FW:(t + 1) * FW], preferred_element_type=F32)
            acc = got if acc is None else acc + got
        uf[...] = acc

        def rows(i):
            at = pl.ds(pl.multiple_of(i * 16, 16), 16)
            g, slope = gelu_parts(uf[at])
            gf[b, at] = g.astype(BF)
            su[b, at] = slope

        loop(PB // 16, rows)
        gg[b, 0] = gf[b, :, mine(0)]
        g_near(b).start()

    def turn(src, dst, b):
        at = pl.ds(pl.multiple_of(b * 2 * PB, 2 * PB), 2 * PB)
        for m in range(NY):
            dst[m, :, at] = src[b, :, :, m * HW:(m + 1) * HW].reshape(2 * PB, HW).T

    def turn_lower(b):
        at = pl.ds(pl.multiple_of(b * 2 * PB, 2 * PB), 2 * PB)
        n_near(b).wait_recv()
        for m in range(NY):
            cols = slice(m * HW, (m + 1) * HW)
            cT[m, :, at] = jnp.concatenate([dnx[b, :, cols], nx[b, :, cols]], axis=0).T

    def turn_own(b):
        for q in range(NQ):
            c_near(b, q).wait_recv()
        turn(ct, tT, b)

    def send_up(b):
        g_near(b).wait_recv()
        g_up(b).start()

    @pl.when(s < NS - 1)
    def _():
        loop(SEQS, forward_mid)
        loop(SEQS, send_up)
        loop(SEQS, lambda b: turn(hx, hT, b))

    def front(b):
        dg = None
        for q in range(NQ):
            @pl.when(s < NS - 1)
            def _():
                hop(b, q).wait_recv()

            got = jnp.dot(ct[b, 0, :, part(q)], wo[q * QW:(q + 1) * QW], preferred_element_type=F32)
            dg = got if dg is None else dg + got
        dux[b] = (dg * su[b]).astype(BF)
        d_far(b, lambda one: one.start())
        d_near(b).start()

    def first_front(b):
        forward_mid(b)
        load_top(b).wait()
        front(b)
        for q in range(NQ):
            c_near(b, q).start()

        @pl.when(b < SEQS - 2)
        def _():
            h_far(b + 2).start()

    def any_front(b, more):
        @pl.when(jnp.logical_and(s < NS - 1, more))
        def _():
            front(b)

        @pl.when(jnp.logical_and(s == NS - 1, more))
        def _():
            first_front(b)

    def input_grad(b):
        for q in range(NQ):
            dh = jnp.dot(dwin[b], wt[:, part(q)], preferred_element_type=F32)
            dnx[b, :, part(q)] = (ct[b, 0, :, part(q)].astype(F32) + dh * gx[b, :, part(q)]).astype(BF)

            @pl.when(s > 0)
            def _():
                hop(b, q).start()

        save(b).start()

        @pl.when(s > 0)
        def _():
            n_near(b).start()

    def backward(b):
        any_front(b + 1, b < SEQS - 1)

        @pl.when(b >= 0)
        def _():
            behind(b)

    def behind(b):
        extd[own_at] = dux[b].astype(F32)
        d_near(b).wait_recv()
        extd[near_at] = dup[b].astype(F32)
        d_far(b, lambda one: one.wait_recv())
        extd[far_at] = jnp.where(edge, 0.0, duo[b].astype(F32))
        for t in range(3):
            at = pl.ds(pl.multiple_of(PB - (t - 1) * d, 8), PB)
            dwin[b, :, t * FW:(t + 1) * FW] = extd[at].astype(BF)
        @pl.when(jnp.logical_or(s > 0, b < SEQS - 1))
        def _():
            input_grad(b)

        for t in range(3):
            w_near(b, t).start()
            dw[b, 0, :, t * HW:(t + 1) * HW] = dwin[b, :, mine(t)]

        @pl.when(b > 0)
        def _():
            turns(b - 1)

    def turns(b):
        @pl.when(s > 0)
        def _():
            turn_lower(b)

        @pl.when(s == NS - 1)
        def _():
            turn_own(b)

    loop(SEQS + 1, lambda i: backward(i - 1))
    turns(SEQS - 1)

    @pl.when(s == NS - 1)
    def _():
        loop(SEQS, lambda b: turn(hx, hT, b))

    def gathered(b):
        for t in range(3):
            w_near(b, t).wait_recv()

        @pl.when(s == NS - 1)
        def _():
            g_near(b).wait_recv()

        @pl.when(s > 0)
        def _():
            g_up(b).wait_recv()

    loop(SEQS, gathered)

    def fill(b, block):
        lhs = {3: cT, 4: tT}.get(b, hT)
        for m in range(NY):
            rhs = gu[...] if b == 3 else gg[...] if b == 4 else dw[:, :, :, b * HW:(b + 1) * HW]
            got = jnp.dot(lhs[m], rhs.reshape(2 * SEQS * PB, HW), preferred_element_type=F32)
            block[m] = got.reshape(NZ, RB, HW)

    def beside():
        @pl.when(s == 0)
        def _():
            input_grad(SEQS - 1)

    rs_run(fill, beside, scale, conv_ref, out_ref, ring_refs)

    def ended(b):
        save(b).wait()
        h_near(b).wait_send()
        h_far(b).wait_send()
        g_near(b).wait_send()
        d_near(b).wait_send()
        d_far(b, lambda one: one.wait_send())
        for t in range(3):
            w_near(b, t).wait_send()

        @pl.when(s == NS - 1)
        def _():
            for q in range(NQ):
                c_near(b, q).wait_send()

        @pl.when(s < NS - 1)
        def _():
            g_up(b).wait_send()

        @pl.when(s > 0)
        def _():
            n_near(b).wait_send()
            for q in range(NQ):
                hop(b, q).wait_send()

    loop(SEQS, ended)


def pass_on(a, b, c, a_out, b_out, c_out):
    a_out[...] = a[...]
    b_out[...] = b[...]
    c_out[...] = c[...]


def body(layer_input, grad_top, w_conv, w_out):
    scale = 1.0 / math.sqrt(SEQS * PB * 2 * NY * NZ)
    scratch = [pltpu.VMEM(shape, kind) for _, shape, kind in NAMES]
    scratch += [pltpu.SemaphoreType.DMA(shape) for _, shape in SEMS]
    scratch += rs_scratch()
    dinput, conv_grad, out_grad = pl.pallas_call(
        functools.partial(step_kernel, scale),
        out_shape=(
            jax.ShapeDtypeStruct((1, SEQS, PB, CH), BF),
            jax.ShapeDtypeStruct((CH // (2 * NY * NZ), 3 * FW), F32),
            jax.ShapeDtypeStruct((CH // (2 * NY * NZ), FW), F32),
        ),
        in_specs=[pl.BlockSpec(memory_space=pl.ANY)] * 4,
        out_specs=(
            pl.BlockSpec(memory_space=pl.ANY),
            pl.BlockSpec(memory_space=pltpu.VMEM),
            pl.BlockSpec(memory_space=pltpu.VMEM),
        ),
        scratch_shapes=scratch,
        compiler_params=pltpu.CompilerParams(collective_id=1, has_side_effects=True, vmem_limit_bytes=63 << 20),
    )(layer_input, grad_top, w_conv, w_out)
    results = (dinput, conv_grad[None], out_grad[None])
    return pl.pallas_call(
        pass_on,
        out_shape=tuple(jax.ShapeDtypeStruct(one.shape, one.dtype) for one in results),
        in_specs=[pl.BlockSpec(memory_space=pltpu.VMEM)] * 3,
        out_specs=(pl.BlockSpec(memory_space=pltpu.VMEM),) * 3,
    )(*results)


def solution(mesh):
    return jax.shard_map(
        body,
        mesh=mesh,
        in_specs=(
            P("section", None, "seq", None),
            P(None, "seq", None),
            P("section", None, None),
            P("section", None, None),
        ),
        out_specs=(
            P("section", None, "seq", None),
            P("section", "seq", None),
            P("section", "seq", None),
        ),
        check_vma=False,
    )
```
